32 devices in a mesh: row: 4 (over y, core), col: 8 (over z, x).
Axes of the slice: x: 2, y: 2, z: 4, core: 2. Of those that a mesh axis runs over, the one named last changes fastest.
Arguments:
- images: float32 [4, 128, 16384], P(None, 'row', 'col'), may hold values from -6 to 6
Outputs:
- coefficients: float32 [4, 128, 16384], P(None, 'row', 'col')
The draws below stay inside these ranges and needn't reach their ends.
All inputs are finite; a program needn't handle non-finite values.
Results may differ from the reference program's by a relative error of at most 0.00002.
Values sent between devices are 32-bit elements; how exact they have to be, the bound alone decides.
A program may use at most 128 MiB of HBM per device.

```python
import jax
import jax.numpy as jnp
from jax import lax

IMAGES = 4
LEVELS = 3
NR = 128
NC = 16384


def steps_of(key, extent, cuts, low, high):
    def one(dim, parts):
        steps = jax.random.uniform(jax.random.fold_in(jax.random.fold_in(key, 6), dim), (parts,), jnp.float32, low / len(cuts), high / len(cuts))
        return jnp.repeat(jnp.exp(steps), extent[dim] // parts).reshape((-1,) + (1,) * (len(extent) - dim - 1))

    loudness = one(*cuts[0])
    for cut in cuts[1:]:
        loudness = loudness * one(*cut)
    return loudness


def normal_values(stream_key, dims, scale, most, shards=(), kind=jnp.bfloat16):
    values = scale * jax.random.normal(stream_key, dims, jnp.float32)
    if shards:
        values = values * steps_of(stream_key, dims, shards, -0.22, 0.18)
    return jnp.clip(values, -most, most).astype(kind)


def setup_inputs(seed: int = 0) -> dict:
    key_list = jax.random.split(jax.random.key(seed), 2)
    images = normal_values(key_list[0], (IMAGES, NR, NC), 1.0, 6.0, ((1, 4), (2, 8)), jnp.float32)
    return dict(images=images)


PREDICT_ONE = -1.586134342
UPDATE_ONE = -0.05298011854
PREDICT_TWO = 0.8829110762
UPDATE_TWO = 0.4435068522
SCALE_HIGH = 1.230174105
SCALE_LOW = 1.0 / 1.230174105


def segment(values, start, stop, along):
    return lax.slice_in_dim(values, start, stop, 1, along)


def lifting(extended, along):
    length = extended.shape[along]
    halves = length // 2
    evens = lax.slice_in_dim(extended, 0, length, 2, along)
    odds = lax.slice_in_dim(extended, 1, length, 2, along)
    predicted = segment(odds, 0, halves - 1, along) + PREDICT_ONE * (segment(evens, 0, halves - 1, along) + segment(evens, 1, halves, along))
    updated = segment(evens, 1, halves - 1, along) + UPDATE_ONE * (segment(predicted, 0, halves - 2, along) + segment(predicted, 1, halves - 1, along))
    refined = segment(predicted, 1, halves - 2, along) + PREDICT_TWO * (segment(updated, 0, halves - 3, along) + segment(updated, 1, halves - 2, along))
    smoothed = segment(updated, 1, halves - 3, along) + UPDATE_TWO * (segment(refined, 0, halves - 4, along) + segment(refined, 1, halves - 3, along))
    lowpass = smoothed * SCALE_LOW
    highpass = segment(refined, 1, halves - 3, along) * SCALE_HIGH
    paired = jnp.stack([lowpass, highpass], axis=along + 1)
    shape = list(extended.shape)
    shape[along] = length - 8
    return paired.reshape(shape)


def one_level(lowband):
    extended = jnp.pad(lowband, ((0, 0), (4, 4), (0, 0)), mode="reflect")
    vertical = lifting(extended, 1)
    extended = jnp.pad(vertical, ((0, 0), (0, 0), (4, 4)), mode="reflect")
    return lifting(extended, 2)


def one_image(single):
    lowband = single[None]
    results = []
    for level_index in range(LEVELS):
        transformed = one_level(lowband)
        results.append(transformed)
        lowband = transformed[:, ::2, ::2]
    combined = results[-1]
    for transformed in reversed(results[:-1]):
        combined = transformed.at[:, ::2, ::2].set(combined)
    return combined[0]


def reference(images):
    return lax.map(one_image, images)
```

```python
import functools

import jax
import jax.numpy as jnp
from jax import lax
from jax.experimental import pallas as pl
from jax.experimental.pallas import tpu as pltpu
from jax.sharding import PartitionSpec as P

LEVELS = 3
PREDICT_ONE = -1.586134342
UPDATE_ONE = -0.05298011854
PREDICT_TWO = 0.8829110762
UPDATE_TWO = 0.4435068522
SCALE_HIGH = 1.230174105
SCALE_LOW = 1.0 / 1.230174105
STEPS = (PREDICT_ONE, UPDATE_ONE, PREDICT_TWO, UPDATE_TWO)

SUB, LANE = 8, 128
ABOVE, BELOW = 28, 21


def row_cascade(rows, own, at_top, at_bottom):
    levels = []
    for level in range(LEVELS):
        dist = 1 << level
        for step, factor in enumerate(STEPS):
            first = dist if step % 2 == 0 else 0
            for r in sorted(rows):
                if (r - first) % (2 * dist) or r - dist not in rows or r + dist not in rows:
                    continue
                before, after = rows[r - dist], rows[r + dist]
                if r == 0:
                    before = jnp.where(at_top, after, before)
                if r == own - dist:
                    after = jnp.where(at_bottom, before, after)
                rows[r] = rows[r] + factor * (before + after)
            if step:
                edge = min(rows), max(rows)
                rows = {r: v for r, v in rows.items() if edge[0] < r < edge[1]}
        lows = {r: v * SCALE_LOW for r, v in rows.items() if r % (2 * dist) == 0}
        levels.append({
            r: lows[r] if r % (2 * dist) == 0 else rows[r] * SCALE_HIGH
            for r in range(0, own, dist)
        })
        rows = lows
    return levels


def lane_level(tiles, level, masks):
    dist = 1 << level
    lane, at_left, at_right = masks
    count = len(tiles)
    odd = (lane // dist) % 2 == 1
    low_edge, high_edge = lane < dist, lane >= LANE - dist
    for step, factor in enumerate(STEPS):
        weight = jnp.where(odd if step % 2 == 0 else ~odd, factor, 0.0)
        fwd = [pltpu.roll(t, dist, 1) for t in tiles]
        bwd = [pltpu.roll(t, LANE - dist, 1) for t in tiles]
        fresh = []
        for q in range(count):
            left = jnp.where(low_edge, fwd[q - 1], fwd[q])
            right = jnp.where(high_edge, bwd[(q + 1) % count], bwd[q])
            if q == 1:
                left = jnp.where(at_left & low_edge, right, left)
            if q == count - 1:
                right = jnp.where(at_right & high_edge, left, right)
            fresh.append(tiles[q] + weight * (left + right))
        tiles = fresh
    scale = jnp.where(odd, SCALE_HIGH, SCALE_LOW)
    return [t * scale for t in tiles]


def kernel(nr, nc, x, out, held, done, *rest):
    banks, (send_sem, recv_sem, out_sem) = rest[:LEVELS], rest[LEVELS:]
    images, bands, tiles = x.shape[0], x.shape[1], x.shape[2]
    half = tiles // 2
    width = half + 2
    own = bands * SUB
    below = -(-BELOW // SUB)
    r_at, c_at = lax.axis_index("row"), lax.axis_index("col")

    def inside(dr, dc):
        ok = []
        if dr:
            ok.append(r_at > 0 if dr < 0 else r_at < nr - 1)
        if dc:
            ok.append(c_at > 0 if dc < 0 else c_at < nc - 1)
        return ok[0] if len(ok) == 1 else ok[0] & ok[1]

    around = [(dr, dc) for dr in (-1, 0, 1) for dc in (-1, 0, 1) if dr or dc]
    barrier = pltpu.get_barrier_semaphore()
    total = jnp.int32(0)
    for dr, dc in around:
        ok = inside(dr, dc)
        total = total + ok.astype(jnp.int32)

        @pl.when(ok)
        def _():
            pl.semaphore_signal(
                barrier, inc=1, device_id=(r_at + dr, c_at + dc),
                device_id_type=pl.DeviceIdType.MESH,
            )

    row_part = {
        -1: (pl.ds(0, bands), pl.ds(0, bands)),
        0: (pl.ds(0, bands), pl.ds(bands, bands)),
        1: (pl.ds(0, below), pl.ds(2 * bands, below)),
    }
    col_part = (
        (0, 0, pl.ds(0, half + 1), pl.ds(1, half + 1)),
        (0, 1, pl.ds(half - 1, half + 1), pl.ds(0, half + 1)),
        (-1, 0, pl.ds(tiles - 1, 1), pl.ds(0, 1)),
        (1, 1, pl.ds(0, 1), pl.ds(width - 1, 1)),
    )
    parts = [
        (dr, dc, x.at[:, src_r, src_c], held.at[h, :, dst_r, dst_c])
        for dr, (src_r, dst_r) in row_part.items()
        for dc, h, src_c, dst_c in col_part
    ]

    def local(n):
        return pltpu.make_async_copy(parts[n][2], parts[n][3], recv_sem.at[n])

    def remote(n):
        dr, dc, src, dst = parts[n]
        return pltpu.make_async_remote_copy(
            src_ref=src, dst_ref=dst, send_sem=send_sem.at[n], recv_sem=recv_sem.at[n],
            device_id=(r_at - dr, c_at - dc), device_id_type=pl.DeviceIdType.MESH,
        )

    for n, (dr, dc, _, _) in enumerate(parts):
        if not (dr or dc):
            local(n).start()
    pl.semaphore_wait(barrier, total)
    for n, (dr, dc, _, _) in enumerate(parts):
        if dr or dc:
            @pl.when(inside(-dr, -dc))
            def _():
                remote(n).start()
    for n, (dr, dc, _, _) in enumerate(parts):
        if dr or dc:
            @pl.when(inside(dr, dc))
            def _():
                remote(n).wait_recv()
        else:
            local(n).wait()

    strands = 2 * images
    pitch = (2 * bands + below) * width * SUB
    flat = held.reshape(strands * pitch, LANE)
    lane = lax.broadcasted_iota(jnp.int32, (strands, LANE), 1)
    strand = lax.broadcasted_iota(jnp.int32, (strands, LANE), 0)
    at_top = jnp.broadcast_to(r_at == 0, (strands, LANE))
    at_bottom = jnp.broadcast_to(r_at == nr - 1, (strands, LANE))
    at_left = (strand < images) & (c_at == 0)
    at_right = (strand >= images) & (c_at == nc - 1)

    def fetch(r, t):
        at = r + own
        start = ((at // SUB) * width + t) * SUB + at % SUB
        return flat[pl.ds(start, strands, stride=pitch), :]

    span = range(-ABOVE, own + BELOW)

    def keep(rows, q):
        for level, found in enumerate(row_cascade(rows, own, at_top, at_bottom)):
            for r, value in found.items():
                banks[level][r >> level, q] = value

    keep({r: jnp.where(lane < LANE // 2, fetch(r, width - 1), fetch(r, 0)) for r in span}, 0)

    def columns(q, carry):
        keep({r: fetch(r, q) for r in span}, q)
        return carry

    lax.fori_loop(1, half + 1, columns, 0)

    masks = (lane, at_left, at_right)
    stretch = bands * half * SUB
    target = done.reshape(strands * stretch, LANE)
    group = 1 << (LEVELS - 1)

    def bundle(i, carry):
        for k in range(group):
            r = i * group + k
            result = None
            for level in range(LEVELS):
                if k % (1 << level):
                    break
                row = i * (group >> level) + (k >> level)
                value = [banks[level][row, q] for q in range(half + 1)]
                for lower in range(level + 1):
                    value = lane_level(value, lower, masks)
                result = value if result is None else [
                    jnp.where(lane % (1 << level) == 0, new, old)
                    for new, old in zip(value, result)
                ]
            for q in range(half):
                start = ((r // SUB) * half + q) * SUB + r % SUB
                target[pl.ds(start, strands, stride=stretch), :] = result[q + 1]
        return carry

    lax.fori_loop(0, own // group, bundle, 0)

    copies = [
        pltpu.make_async_copy(done.at[h], out.at[:, :, pl.ds(h * half, half)], out_sem.at[h])
        for h in range(2)
    ]
    for copy in copies:
        copy.start()
    for n, (dr, dc, _, _) in enumerate(parts):
        if dr or dc:
            @pl.when(inside(-dr, -dc))
            def _():
                remote(n).wait_send()
    for copy in copies:
        copy.wait()


def shards(nr, nc, block):
    images, own, cols = block.shape
    bands, tiles = own // SUB, cols // LANE
    half = tiles // 2
    below = -(-BELOW // SUB)
    x = block.reshape(images, bands, SUB, tiles, LANE).transpose(0, 1, 3, 2, 4)
    y = pl.pallas_call(
        functools.partial(kernel, nr, nc),
        out_shape=jax.ShapeDtypeStruct(x.shape, x.dtype),
        in_specs=[pl.BlockSpec(memory_space=pl.ANY)],
        out_specs=pl.BlockSpec(memory_space=pl.ANY),
        scratch_shapes=[
            pltpu.VMEM((2, images, 2 * bands + below, half + 2, SUB, LANE), jnp.float32),
            pltpu.VMEM((2, images, bands, half, SUB, LANE), jnp.float32),
            *[pltpu.VMEM((own >> n, half + 1, 2 * images, LANE), jnp.float32) for n in range(LEVELS)],
            pltpu.SemaphoreType.DMA((12,)),
            pltpu.SemaphoreType.DMA((12,)),
            pltpu.SemaphoreType.DMA((2,)),
        ],
        compiler_params=pltpu.CompilerParams(collective_id=0, has_side_effects=True, vmem_limit_bytes=40 << 20),
    )(x)
    return y.transpose(0, 1, 3, 2, 4).reshape(images, own, cols)


def solution(mesh):
    return jax.shard_map(
        functools.partial(shards, mesh.shape["row"], mesh.shape["col"]),
        mesh=mesh,
        in_specs=(P(None, "row", "col"),),
        out_specs=P(None, "row", "col"),
        check_vma=False,
    )
```

```python
import functools

import jax
import jax.numpy as jnp
from jax import lax
from jax.experimental import pallas as pl
from jax.experimental.pallas import tpu as pltpu
from jax.sharding import PartitionSpec as P

LEVELS = 3
PREDICT_ONE = -1.586134342
UPDATE_ONE = -0.05298011854
PREDICT_TWO = 0.8829110762
UPDATE_TWO = 0.4435068522
SCALE_HIGH = 1.230174105
SCALE_LOW = 1.0 / 1.230174105
STEPS = (PREDICT_ONE, UPDATE_ONE, PREDICT_TWO, UPDATE_TWO)

SUB, LANE = 8, 128
REACH = 4


def row_level(rows, count, at_top, at_bottom):
    rows = dict(rows)
    for step, factor in enumerate(STEPS):
        for r in range(-REACH + 1 + step, count + REACH - 2 - step, 2):
            before, after = rows[r - 1], rows[r + 1]
            if r == 0:
                before = jnp.where(at_top, after, before)
            if r == count - 1:
                after = jnp.where(at_bottom, before, after)
            rows[r] = rows[r] + factor * (before + after)
    return [rows[r] * (SCALE_HIGH if r % 2 else SCALE_LOW) for r in range(count)]


def lane_level(tiles, level, masks):
    dist = 1 << level
    lane, at_left, at_right = masks
    count = len(tiles)
    odd = (lane // dist) % 2 == 1
    low_edge, high_edge = lane < dist, lane >= LANE - dist
    for step, factor in enumerate(STEPS):
        weight = jnp.where(odd if step % 2 == 0 else ~odd, factor, 0.0)
        fwd = [pltpu.roll(t, dist, 1) for t in tiles]
        bwd = [pltpu.roll(t, LANE - dist, 1) for t in tiles]
        fresh = []
        for q in range(count):
            left = jnp.where(low_edge, fwd[q - 1], fwd[q])
            right = jnp.where(high_edge, bwd[(q + 1) % count], bwd[q])
            if q == 1:
                left = jnp.where(at_left & low_edge, right, left)
            if q == count - 1:
                right = jnp.where(at_right & high_edge, left, right)
            fresh.append(tiles[q] + weight * (left + right))
        tiles = fresh
    scale = jnp.where(odd, SCALE_HIGH, SCALE_LOW)
    return [t * scale for t in tiles]


def kernel(nr, nc, x, out, held, done, *rest):
    banks, rest = rest[:LEVELS], rest[LEVELS:]
    edges, (send_sem, recv_sem, out_sem) = rest[:-3], rest[-3:]
    images, bands, tiles = x.shape[0], x.shape[1], x.shape[2]
    half = tiles // 2
    width = half + 2
    own = bands * SUB
    r_at, c_at = lax.axis_index("row"), lax.axis_index("col")

    def inside(dr, dc):
        ok = []
        if dr:
            ok.append(r_at > 0 if dr < 0 else r_at < nr - 1)
        if dc:
            ok.append(c_at > 0 if dc < 0 else c_at < nc - 1)
        return ok[0] if len(ok) == 1 else ok[0] & ok[1]

    around = [(dr, dc) for dr in (-1, 0, 1) for dc in (-1, 0, 1) if dr or dc]
    barrier = pltpu.get_barrier_semaphore()
    total = jnp.int32(0)
    for dr, dc in around:
        ok = inside(dr, dc)
        total = total + ok.astype(jnp.int32)

        @pl.when(ok)
        def _():
            pl.semaphore_signal(
                barrier, inc=1, device_id=(r_at + dr, c_at + dc),
                device_id_type=pl.DeviceIdType.MESH,
            )

    row_part = {
        -1: (pl.ds(bands - 1, 1), pl.ds(0, 1)),
        0: (pl.ds(0, bands), pl.ds(1, bands)),
        1: (pl.ds(0, 1), pl.ds(bands + 1, 1)),
    }
    col_part = (
        (0, 0, pl.ds(0, half + 1), pl.ds(1, half + 1)),
        (0, 1, pl.ds(half - 1, half + 1), pl.ds(0, half + 1)),
        (-1, 0, pl.ds(tiles - 1, 1), pl.ds(0, 1)),
        (1, 1, pl.ds(0, 1), pl.ds(width - 1, 1)),
    )
    parts = [
        (dr, dc, x.at[:, src_r, src_c], held.at[h, :, dst_r, dst_c])
        for dr, (src_r, dst_r) in row_part.items()
        for dc, h, src_c, dst_c in col_part
    ]

    def local(n):
        return pltpu.make_async_copy(parts[n][2], parts[n][3], recv_sem.at[n])

    def remote(n):
        dr, dc, src, dst = parts[n]
        return pltpu.make_async_remote_copy(
            src_ref=src, dst_ref=dst, send_sem=send_sem.at[n], recv_sem=recv_sem.at[n],
            device_id=(r_at - dr, c_at - dc), device_id_type=pl.DeviceIdType.MESH,
        )

    for n, (dr, dc, _, _) in enumerate(parts):
        if not (dr or dc):
            local(n).start()
    pl.semaphore_wait(barrier, total)
    for n, (dr, dc, _, _) in enumerate(parts):
        if dr or dc:
            @pl.when(inside(-dr, -dc))
            def _():
                remote(n).start()
    for n, (dr, dc, _, _) in enumerate(parts):
        if dr or dc:
            @pl.when(inside(dr, dc))
            def _():
                remote(n).wait_recv()
        else:
            local(n).wait()

    strands = 2 * images
    pitch = (bands + 2) * width * SUB
    flat = held.reshape(strands * pitch, LANE)
    lane = lax.broadcasted_iota(jnp.int32, (strands, LANE), 1)
    strand = lax.broadcasted_iota(jnp.int32, (strands, LANE), 0)
    at_top = jnp.broadcast_to(r_at == 0, (strands, LANE))
    at_bottom = jnp.broadcast_to(r_at == nr - 1, (strands, LANE))
    at_left = (strand < images) & (c_at == 0)
    at_right = (strand >= images) & (c_at == nc - 1)
    masks = (lane, at_left, at_right)
    stretch = bands * half * SUB
    target = done.reshape(strands * stretch, LANE)

    def fetch(r, t):
        at = r + SUB
        start = ((at // SUB) * width + t) * SUB + at % SUB
        return flat[pl.ds(start, strands, stride=pitch), :]

    def keep(level, rows, q):
        count = own >> level
        found = row_level(rows, count, at_top, at_bottom)
        for r, value in enumerate(found):
            banks[level][r, q] = value
        if level < LEVELS - 1:
            lows = found[::2]
            up, down = edges[4 * level], edges[4 * level + 1]
            for r in range(REACH - 1):
                up[r, q] = lows[r]
            for r in range(REACH):
                down[r, q] = lows[len(lows) - REACH + r]

    def passing(level, n):
        at = 12 + 2 * level + n
        return pltpu.make_async_remote_copy(
            src_ref=edges[4 * level + n], dst_ref=edges[4 * level + 2 + n],
            send_sem=send_sem.at[at], recv_sem=recv_sem.at[at],
            device_id=(r_at - 1 + 2 * n, c_at), device_id_type=pl.DeviceIdType.MESH,
        )

    def send(level):
        for n in range(2):
            @pl.when(inside(2 * n - 1, 0))
            def _():
                passing(level, n).start()

    def receive(level):
        for n in range(2):
            @pl.when(inside(1 - 2 * n, 0))
            def _():
                passing(level, n).wait_recv()

    span = range(-REACH, own + REACH - 1)
    keep(0, {r: jnp.where(lane < LANE // 2, fetch(r, width - 1), fetch(r, 0)) for r in span}, 0)

    def first_rows(q, carry):
        keep(0, {r: fetch(r, q) for r in span}, q)
        return carry

    lax.fori_loop(1, half + 1, first_rows, 0)

    for level in range(LEVELS):
        dist = 1 << level
        if level < LEVELS - 1:
            send(level)

        def lanes(i, carry):
            for k in range(2):
                row = 2 * i + k
                value = [banks[level][row, q] for q in range(half + 1)]
                for lower in range(level + 1):
                    value = lane_level(value, lower, masks)
                r = row * dist
                for q in range(half):
                    start = ((r // SUB) * half + q) * SUB + r % SUB
                    at = pl.ds(start, strands, stride=stretch)
                    new = value[q + 1]
                    if level:
                        new = jnp.where(lane % dist == 0, new, target[at, :])
                    target[at, :] = new
            return carry

        lax.fori_loop(0, (own >> level) // 2, lanes, 0)
        if level < LEVELS - 1:
            receive(level)
            count = own >> (level + 1)

            def next_rows(q, carry):
                rows = {r: banks[level][2 * r, q] for r in range(count)}
                for r in range(REACH):
                    rows[r - REACH] = edges[4 * level + 3][r, q]
                for r in range(REACH - 1):
                    rows[count + r] = edges[4 * level + 2][r, q]
                keep(level + 1, rows, q)
                return carry

            lax.fori_loop(0, half + 1, next_rows, 0)

    copies = [
        pltpu.make_async_copy(done.at[h], out.at[:, :, pl.ds(h * half, half)], out_sem.at[h])
        for h in range(2)
    ]
    for copy in copies:
        copy.start()
    for n, (dr, dc, _, _) in enumerate(parts):
        if dr or dc:
            @pl.when(inside(-dr, -dc))
            def _():
                remote(n).wait_send()
    for level in range(LEVELS - 1):
        for n in range(2):
            @pl.when(inside(2 * n - 1, 0))
            def _():
                passing(level, n).wait_send()
    for copy in copies:
        copy.wait()


def shards(nr, nc, block):
    images, own, cols = block.shape
    bands, tiles = own // SUB, cols // LANE
    half = tiles // 2
    x = block.reshape(images, bands, SUB, tiles, LANE).transpose(0, 1, 3, 2, 4)
    y = pl.pallas_call(
        functools.partial(kernel, nr, nc),
        out_shape=jax.ShapeDtypeStruct(x.shape, x.dtype),
        in_specs=[pl.BlockSpec(memory_space=pl.ANY)],
        out_specs=pl.BlockSpec(memory_space=pl.ANY),
        scratch_shapes=[
            pltpu.VMEM((2, images, bands + 2, half + 2, SUB, LANE), jnp.float32),
            pltpu.VMEM((2, images, bands, half, SUB, LANE), jnp.float32),
            *[pltpu.VMEM((own >> n, half + 1, 2 * images, LANE), jnp.float32) for n in range(LEVELS)],
            *[
                pltpu.VMEM((n, half + 1, 2 * images, LANE), jnp.float32)
                for n in (REACH - 1, REACH) * (2 * (LEVELS - 1))
            ],
            pltpu.SemaphoreType.DMA((12 + 2 * (LEVELS - 1),)),
            pltpu.SemaphoreType.DMA((12 + 2 * (LEVELS - 1),)),
            pltpu.SemaphoreType.DMA((2,)),
        ],
        compiler_params=pltpu.CompilerParams(collective_id=0, has_side_effects=True, vmem_limit_bytes=40 << 20),
    )(x)
    return y.transpose(0, 1, 3, 2, 4).reshape(images, own, cols)


def solution(mesh):
    return jax.shard_map(
        functools.partial(shards, mesh.shape["row"], mesh.shape["col"]),
        mesh=mesh,
        in_specs=(P(None, "row", "col"),),
        out_specs=P(None, "row", "col"),
        check_vma=False,
    )
```

```python
import functools

import jax
import jax.numpy as jnp
from jax import lax
from jax.experimental import pallas as pl
from jax.experimental.pallas import tpu as pltpu
from jax.sharding import PartitionSpec as P

LEVELS = 3
PREDICT_ONE = -1.586134342
UPDATE_ONE = -0.05298011854
PREDICT_TWO = 0.8829110762
UPDATE_TWO = 0.4435068522
SCALE_HIGH = 1.230174105
SCALE_LOW = 1.0 / 1.230174105
STEPS = (PREDICT_ONE, UPDATE_ONE, PREDICT_TWO, UPDATE_TWO)

SUB, LANE = 8, 128
REACH = 4

TRIPS = (8, 8, 8)


def row_level(rows, count, at_top, at_bottom):
    rows = dict(rows)
    for step, factor in enumerate(STEPS):
        for r in range(-REACH + 1 + step, count + REACH - 2 - step, 2):
            before, after = rows[r - 1], rows[r + 1]
            if r == 0:
                before = jnp.where(at_top, after, before)
            if r == count - 1:
                after = jnp.where(at_bottom, before, after)
            rows[r] = rows[r] + factor * (before + after)
    return [rows[r] * (SCALE_HIGH if r % 2 else SCALE_LOW) for r in range(count)]


def lane_level(group, level, masks):
    dist = 1 << level
    lane, at_left, at_right = masks
    odd = (lane // dist) % 2 == 1
    low_edge, high_edge = lane < dist, lane >= LANE - dist
    mirror_left, mirror_right = at_left & low_edge, at_right & high_edge
    for step, factor in enumerate(STEPS):
        weight = jnp.where(odd if step % 2 == 0 else ~odd, factor, 0.0)
        moved = []
        for tiles in group:
            count = len(tiles)
            fwd = [pltpu.roll(t, dist, 1) for t in tiles]
            bwd = [pltpu.roll(t, LANE - dist, 1) for t in tiles]
            fresh = []
            for q in range(count):
                left = jnp.where(low_edge, fwd[q - 1], fwd[q])
                right = jnp.where(high_edge, bwd[(q + 1) % count], bwd[q])
                if q == 1:
                    left = jnp.where(mirror_left, right, left)
                if q == count - 1:
                    right = jnp.where(mirror_right, left, right)
                fresh.append(tiles[q] + weight * (left + right))
            moved.append(fresh)
        group = moved
    scale = jnp.where(odd, SCALE_HIGH, SCALE_LOW)
    return [[t * scale for t in tiles] for tiles in group]


def kernel(nr, nc, x, out, held, done, *rest):
    banks, rest = rest[:LEVELS], rest[LEVELS:]
    edges, (send_sem, recv_sem, out_sem) = rest[:-3], rest[-3:]
    images, bands, tiles = x.shape[0], x.shape[1], x.shape[2]
    half = tiles // 2
    width = half + 2
    own = bands * SUB
    r_at, c_at = lax.axis_index("row"), lax.axis_index("col")

    def inside(dr, dc):
        ok = []
        if dr:
            ok.append(r_at > 0 if dr < 0 else r_at < nr - 1)
        if dc:
            ok.append(c_at > 0 if dc < 0 else c_at < nc - 1)
        return ok[0] if len(ok) == 1 else ok[0] & ok[1]

    around = [(dr, dc) for dr in (-1, 0, 1) for dc in (-1, 0, 1) if dr or dc]
    barrier = pltpu.get_barrier_semaphore()
    total = jnp.int32(0)
    for dr, dc in around:
        ok = inside(dr, dc)
        total = total + ok.astype(jnp.int32)

        @pl.when(ok)
        def _():
            pl.semaphore_signal(
                barrier, inc=1, device_id=(r_at + dr, c_at + dc),
                device_id_type=pl.DeviceIdType.MESH,
            )

    row_part = {
        -1: (pl.ds(bands - 1, 1), pl.ds(0, 1)),
        0: (pl.ds(0, bands), pl.ds(1, bands)),
        1: (pl.ds(0, 1), pl.ds(bands + 1, 1)),
    }
    col_part = (
        (0, 0, pl.ds(0, half + 1), pl.ds(1, half + 1)),
        (0, 1, pl.ds(half - 1, half + 1), pl.ds(0, half + 1)),
        (-1, 0, pl.ds(tiles - 1, 1), pl.ds(0, 1)),
        (1, 1, pl.ds(0, 1), pl.ds(width - 1, 1)),
    )
    parts = [
        (dr, dc, x.at[:, src_r, src_c], held.at[h, :, dst_r, dst_c])
        for dr, (src_r, dst_r) in row_part.items()
        for dc, h, src_c, dst_c in col_part
    ]

    def local(n):
        return pltpu.make_async_copy(parts[n][2], parts[n][3], recv_sem.at[n])

    def remote(n):
        dr, dc, src, dst = parts[n]
        return pltpu.make_async_remote_copy(
            src_ref=src, dst_ref=dst, send_sem=send_sem.at[n], recv_sem=recv_sem.at[n],
            device_id=(r_at - dr, c_at - dc), device_id_type=pl.DeviceIdType.MESH,
        )

    for n, (dr, dc, _, _) in enumerate(parts):
        if not (dr or dc):
            local(n).start()
    pl.semaphore_wait(barrier, total)
    for n, (dr, dc, _, _) in enumerate(parts):
        if dr or dc:
            @pl.when(inside(-dr, -dc))
            def _():
                remote(n).start()
    for n, (dr, dc, _, _) in enumerate(parts):
        if dr or dc:
            @pl.when(inside(dr, dc))
            def _():
                remote(n).wait_recv()
        else:
            local(n).wait()

    strands = 2 * images
    pitch = (bands + 2) * width * SUB
    flat = held.reshape(strands * pitch, LANE)
    lane = lax.broadcasted_iota(jnp.int32, (strands, LANE), 1)
    strand = lax.broadcasted_iota(jnp.int32, (strands, LANE), 0)
    at_top = jnp.broadcast_to(r_at == 0, (strands, LANE))
    at_bottom = jnp.broadcast_to(r_at == nr - 1, (strands, LANE))
    at_left = (strand < images) & (c_at == 0)
    at_right = (strand >= images) & (c_at == nc - 1)
    masks = (lane, at_left, at_right)
    stretch = bands * half * SUB
    target = done.reshape(strands * stretch, LANE)

    def fetch(r, t):
        at = r + SUB
        start = ((at // SUB) * width + t) * SUB + at % SUB
        return flat[pl.ds(start, strands, stride=pitch), :]

    def keep(level, rows, q):
        count = own >> level
        found = row_level(rows, count, at_top, at_bottom)
        for r, value in enumerate(found):
            banks[level][r, q] = value
        if level < LEVELS - 1:
            lows = found[::2]
            up, down = edges[4 * level], edges[4 * level + 1]
            for r in range(REACH - 1):
                up[r, q] = lows[r]
            for r in range(REACH):
                down[r, q] = lows[len(lows) - REACH + r]

    def passing(level, n):
        at = 12 + 2 * level + n
        return pltpu.make_async_remote_copy(
            src_ref=edges[4 * level + n], dst_ref=edges[4 * level + 2 + n],
            send_sem=send_sem.at[at], recv_sem=recv_sem.at[at],
            device_id=(r_at - 1 + 2 * n, c_at), device_id_type=pl.DeviceIdType.MESH,
        )

    def send(level):
        for n in range(2):
            @pl.when(inside(2 * n - 1, 0))
            def _():
                passing(level, n).start()

    def receive(level):
        for n in range(2):
            @pl.when(inside(1 - 2 * n, 0))
            def _():
                passing(level, n).wait_recv()

    span = range(-REACH, own + REACH - 1)
    keep(0, {r: jnp.where(lane < LANE // 2, fetch(r, width - 1), fetch(r, 0)) for r in span}, 0)

    def first_rows(q, carry):
        keep(0, {r: fetch(r, q) for r in span}, q)
        return carry

    lax.fori_loop(1, half + 1, first_rows, 0)

    for level in range(LEVELS):
        dist = 1 << level
        trip = TRIPS[level]
        if level < LEVELS - 1:
            send(level)

        def lanes(i, carry):
            group = [
                [banks[level][trip * i + k, q] for q in range(half + 1)] for k in range(trip)
            ]
            for lower in range(level + 1):
                group = lane_level(group, lower, masks)
            for k in range(trip):
                r = (trip * i + k) * dist
                for q in range(half):
                    start = ((r // SUB) * half + q) * SUB + r % SUB
                    at = pl.ds(start, strands, stride=stretch)
                    new = group[k][q + 1]
                    if level:
                        new = jnp.where(lane % dist == 0, new, target[at, :])
                    target[at, :] = new
            return carry

        lax.fori_loop(0, (own >> level) // trip, lanes, 0)
        if level < LEVELS - 1:
            receive(level)
            count = own >> (level + 1)

            def next_rows(q, carry):
                rows = {r: banks[level][2 * r, q] for r in range(count)}
                for r in range(REACH):
                    rows[r - REACH] = edges[4 * level + 3][r, q]
                for r in range(REACH - 1):
                    rows[count + r] = edges[4 * level + 2][r, q]
                keep(level + 1, rows, q)
                return carry

            lax.fori_loop(0, half + 1, next_rows, 0)

    copies = [
        pltpu.make_async_copy(done.at[h], out.at[:, :, pl.ds(h * half, half)], out_sem.at[h])
        for h in range(2)
    ]
    for copy in copies:
        copy.start()
    for n, (dr, dc, _, _) in enumerate(parts):
        if dr or dc:
            @pl.when(inside(-dr, -dc))
            def _():
                remote(n).wait_send()
    for level in range(LEVELS - 1):
        for n in range(2):
            @pl.when(inside(2 * n - 1, 0))
            def _():
                passing(level, n).wait_send()
    for copy in copies:
        copy.wait()


def shards(nr, nc, block):
    images, own, cols = block.shape
    bands, tiles = own // SUB, cols // LANE
    half = tiles // 2
    x = block.reshape(images, bands, SUB, tiles, LANE).transpose(0, 1, 3, 2, 4)
    y = pl.pallas_call(
        functools.partial(kernel, nr, nc),
        out_shape=jax.ShapeDtypeStruct(x.shape, x.dtype),
        in_specs=[pl.BlockSpec(memory_space=pl.ANY)],
        out_specs=pl.BlockSpec(memory_space=pl.ANY),
        scratch_shapes=[
            pltpu.VMEM((2, images, bands + 2, half + 2, SUB, LANE), jnp.float32),
            pltpu.VMEM((2, images, bands, half, SUB, LANE), jnp.float32),
            *[pltpu.VMEM((own >> n, half + 1, 2 * images, LANE), jnp.float32) for n in range(LEVELS)],
            *[
                pltpu.VMEM((n, half + 1, 2 * images, LANE), jnp.float32)
                for n in (REACH - 1, REACH) * (2 * (LEVELS - 1))
            ],
            pltpu.SemaphoreType.DMA((12 + 2 * (LEVELS - 1),)),
            pltpu.SemaphoreType.DMA((12 + 2 * (LEVELS - 1),)),
            pltpu.SemaphoreType.DMA((2,)),
        ],
        compiler_params=pltpu.CompilerParams(collective_id=0, has_side_effects=True, vmem_limit_bytes=40 << 20),
    )(x)
    return y.transpose(0, 1, 3, 2, 4).reshape(images, own, cols)


def solution(mesh):
    return jax.shard_map(
        functools.partial(shards, mesh.shape["row"], mesh.shape["col"]),
        mesh=mesh,
        in_specs=(P(None, "row", "col"),),
        out_specs=P(None, "row", "col"),
        check_vma=False,
    )
```

```python
import functools

import jax
import jax.numpy as jnp
from jax import lax
from jax.experimental import pallas as pl
from jax.experimental.pallas import tpu as pltpu
from jax.sharding import PartitionSpec as P

LEVELS = 3
PREDICT_ONE = -1.586134342
UPDATE_ONE = -0.05298011854
PREDICT_TWO = 0.8829110762
UPDATE_TWO = 0.4435068522
SCALE_HIGH = 1.230174105
SCALE_LOW = 1.0 / 1.230174105
STEPS = (PREDICT_ONE, UPDATE_ONE, PREDICT_TWO, UPDATE_TWO)

SUB, LANE = 8, 128
REACH = 4

TRIPS = (16, 16, 8)


def row_level(rows, count, at_top, at_bottom):
    rows = dict(rows)
    for step, factor in enumerate(STEPS):
        for r in range(-REACH + 1 + step, count + REACH - 2 - step, 2):
            before, after = rows[r - 1], rows[r + 1]
            if r == 0:
                before = jnp.where(at_top, after, before)
            if r == count - 1:
                after = jnp.where(at_bottom, before, after)
            rows[r] = rows[r] + factor * (before + after)
    return [rows[r] * (SCALE_HIGH if r % 2 else SCALE_LOW) for r in range(count)]


def lane_levels(group, level, last, masks):
    dist = 1 << level
    lane, at_left, at_right = masks
    first = (lane & dist) == 0
    head, tail = lane < 2 * dist, lane >= LANE - 2 * dist
    mirror_left, mirror_right = at_left & head, at_right & tail
    count = len(group[0])

    def up(t, by):
        return pltpu.roll(t, by, 1)

    def down(t, by):
        return pltpu.roll(t, LANE - by, 1)

    pairs = list(zip(group[::2], group[1::2]))
    even = [[jnp.where(first, x, up(y, dist)) for x, y in zip(*p)] for p in pairs]
    odd = [[jnp.where(first, down(x, dist), y) for x, y in zip(*p)] for p in pairs]
    for step, factor in enumerate(STEPS):
        if step % 2 == 0:
            for s, d in zip(even, odd):
                far = [down(t, 2 * dist) for t in s]
                for q in range(count):
                    after = jnp.where(tail, far[(q + 1) % count], far[q])
                    if q == count - 1:
                        after = jnp.where(mirror_right, s[q], after)
                    d[q] = d[q] + factor * (s[q] + after)
        else:
            for s, d in zip(even, odd):
                far = [up(t, 2 * dist) for t in d]
                for q in range(count):
                    before = jnp.where(head, far[q - 1], far[q])
                    if q == 1:
                        before = jnp.where(mirror_left, d[q], before)
                    s[q] = s[q] + factor * (before + d[q])
    even = [[t * SCALE_LOW for t in s] for s in even]
    result = []
    if level < last:
        for s in lane_levels(even, level + 1, last, masks):
            result += [s, [down(t, dist) for t in s]]
        return result
    for s, d in zip(even, odd):
        d = [t * SCALE_HIGH for t in d]
        result.append([jnp.where(first, x, up(y, dist)) for x, y in zip(s, d)])
        result.append([jnp.where(first, down(x, dist), y) for x, y in zip(s, d)])
    return result


def kernel(nr, nc, x, out, held, done, *rest):
    banks, rest = rest[:LEVELS], rest[LEVELS:]
    edges, (send_sem, recv_sem, out_sem) = rest[:-3], rest[-3:]
    images, bands, tiles = x.shape[0], x.shape[1], x.shape[2]
    half = tiles // 2
    width = half + 2
    own = bands * SUB
    r_at, c_at = lax.axis_index("row"), lax.axis_index("col")

    def inside(dr, dc):
        ok = []
        if dr:
            ok.append(r_at > 0 if dr < 0 else r_at < nr - 1)
        if dc:
            ok.append(c_at > 0 if dc < 0 else c_at < nc - 1)
        return ok[0] if len(ok) == 1 else ok[0] & ok[1]

    around = [(dr, dc) for dr in (-1, 0, 1) for dc in (-1, 0, 1) if dr or dc]
    barrier = pltpu.get_barrier_semaphore()
    total = jnp.int32(0)
    for dr, dc in around:
        ok = inside(dr, dc)
        total = total + ok.astype(jnp.int32)

        @pl.when(ok)
        def _():
            pl.semaphore_signal(
                barrier, inc=1, device_id=(r_at + dr, c_at + dc),
                device_id_type=pl.DeviceIdType.MESH,
            )

    row_part = {
        -1: (pl.ds(bands - 1, 1), pl.ds(0, 1), pl.ds(SUB - REACH, REACH)),
        0: (pl.ds(0, bands), pl.ds(1, bands), pl.ds(0, SUB)),
        1: (pl.ds(0, 1), pl.ds(bands + 1, 1), pl.ds(0, REACH)),
    }
    col_part = (
        (0, 0, pl.ds(0, half + 1), pl.ds(1, half + 1)),
        (0, 1, pl.ds(half - 1, half + 1), pl.ds(0, half + 1)),
        (-1, 0, pl.ds(tiles - 1, 1), pl.ds(0, 1)),
        (1, 1, pl.ds(0, 1), pl.ds(width - 1, 1)),
    )
    parts = [
        (dr, dc, x.at[:, src_r, src_c, subs], held.at[h, :, dst_r, dst_c, subs])
        for dr, (src_r, dst_r, subs) in row_part.items()
        for dc, h, src_c, dst_c in col_part
    ]

    def local(n):
        return pltpu.make_async_copy(parts[n][2], parts[n][3], recv_sem.at[n])

    def remote(n):
        dr, dc, src, dst = parts[n]
        return pltpu.make_async_remote_copy(
            src_ref=src, dst_ref=dst, send_sem=send_sem.at[n], recv_sem=recv_sem.at[n],
            device_id=(r_at - dr, c_at - dc), device_id_type=pl.DeviceIdType.MESH,
        )

    for n, (dr, dc, _, _) in enumerate(parts):
        if not (dr or dc):
            local(n).start()
    pl.semaphore_wait(barrier, total)
    order = sorted(range(len(parts)), key=lambda n: parts[n][1] != 0)
    for n in order:
        dr, dc = parts[n][:2]
        if dr or dc:
            @pl.when(inside(-dr, -dc))
            def _():
                remote(n).start()
    for n, (dr, dc, _, _) in enumerate(parts):
        if dr or dc:
            @pl.when(inside(dr, dc))
            def _():
                remote(n).wait_recv()
        else:
            local(n).wait()

    strands = 2 * images
    pitch = (bands + 2) * width * SUB
    flat = held.reshape(strands * pitch, LANE)
    lane = lax.broadcasted_iota(jnp.int32, (strands, LANE), 1)
    strand = lax.broadcasted_iota(jnp.int32, (strands, LANE), 0)
    at_top = jnp.broadcast_to(r_at == 0, (strands, LANE))
    at_bottom = jnp.broadcast_to(r_at == nr - 1, (strands, LANE))
    at_left = (strand < images) & (c_at == 0)
    at_right = (strand >= images) & (c_at == nc - 1)
    masks = (lane, at_left, at_right)
    stretch = bands * half * SUB
    target = done.reshape(strands * stretch, LANE)

    def fetch(r, t):
        at = r + SUB
        start = ((at // SUB) * width + t) * SUB + at % SUB
        return flat[pl.ds(start, strands, stride=pitch), :]

    def keep(level, rows, q):
        count = own >> level
        found = row_level(rows, count, at_top, at_bottom)
        for r, value in enumerate(found):
            banks[level][r, q] = value
        if level < LEVELS - 1:
            lows = found[::2]
            up, down = edges[4 * level], edges[4 * level + 1]
            for r in range(REACH - 1):
                up[r, q] = lows[r]
            for r in range(REACH):
                down[r, q] = lows[len(lows) - REACH + r]

    def passing(level, n):
        at = 12 + 2 * level + n
        return pltpu.make_async_remote_copy(
            src_ref=edges[4 * level + n], dst_ref=edges[4 * level + 2 + n],
            send_sem=send_sem.at[at], recv_sem=recv_sem.at[at],
            device_id=(r_at - 1 + 2 * n, c_at), device_id_type=pl.DeviceIdType.MESH,
        )

    def send(level):
        for n in range(2):
            @pl.when(inside(2 * n - 1, 0))
            def _():
                passing(level, n).start()

    def receive(level):
        for n in range(2):
            @pl.when(inside(1 - 2 * n, 0))
            def _():
                passing(level, n).wait_recv()

    span = range(-REACH, own + REACH - 1)
    keep(0, {r: jnp.where(lane < LANE // 2, fetch(r, width - 1), fetch(r, 0)) for r in span}, 0)

    def first_rows(q, carry):
        keep(0, {r: fetch(r, q) for r in span}, q)
        return carry

    lax.fori_loop(1, half + 1, first_rows, 0)

    for level in range(LEVELS):
        dist = 1 << level
        trip = TRIPS[level]
        if level < LEVELS - 1:
            send(level)

        def lanes(i, carry):
            group = [
                [banks[level][trip * i + k, q] for q in range(half + 1)] for k in range(trip)
            ]
            group = lane_levels(group, 0, level, masks)
            for k in range(trip):
                r = (trip * i + k) * dist
                for q in range(half):
                    start = ((r // SUB) * half + q) * SUB + r % SUB
                    at = pl.ds(start, strands, stride=stretch)
                    new = group[k][q + 1]
                    if level:
                        new = jnp.where(lane % dist == 0, new, target[at, :])
                    target[at, :] = new
            return carry

        lax.fori_loop(0, (own >> level) // trip, lanes, 0)
        if level < LEVELS - 1:
            receive(level)
            count = own >> (level + 1)

            def next_rows(q, carry):
                rows = {r: banks[level][2 * r, q] for r in range(count)}
                for r in range(REACH):
                    rows[r - REACH] = edges[4 * level + 3][r, q]
                for r in range(REACH - 1):
                    rows[count + r] = edges[4 * level + 2][r, q]
                keep(level + 1, rows, q)
                return carry

            lax.fori_loop(0, half + 1, next_rows, 0)

    copies = [
        pltpu.make_async_copy(done.at[h], out.at[:, :, pl.ds(h * half, half)], out_sem.at[h])
        for h in range(2)
    ]
    for copy in copies:
        copy.start()
    for n, (dr, dc, _, _) in enumerate(parts):
        if dr or dc:
            @pl.when(inside(-dr, -dc))
            def _():
                remote(n).wait_send()
    for level in range(LEVELS - 1):
        for n in range(2):
            @pl.when(inside(2 * n - 1, 0))
            def _():
                passing(level, n).wait_send()
    for copy in copies:
        copy.wait()


def shards(nr, nc, block):
    images, own, cols = block.shape
    bands, tiles = own // SUB, cols // LANE
    half = tiles // 2
    x = block.reshape(images, bands, SUB, tiles, LANE).transpose(0, 1, 3, 2, 4)
    y = pl.pallas_call(
        functools.partial(kernel, nr, nc),
        out_shape=jax.ShapeDtypeStruct(x.shape, x.dtype),
        in_specs=[pl.BlockSpec(memory_space=pltpu.HBM)],
        out_specs=pl.BlockSpec(memory_space=pl.ANY),
        scratch_shapes=[
            pltpu.VMEM((2, images, bands + 2, half + 2, SUB, LANE), jnp.float32),
            pltpu.VMEM((2, images, bands, half, SUB, LANE), jnp.float32),
            *[pltpu.VMEM((own >> n, half + 1, 2 * images, LANE), jnp.float32) for n in range(LEVELS)],
            *[
                pltpu.VMEM((n, half + 1, 2 * images, LANE), jnp.float32)
                for n in (REACH - 1, REACH) * (2 * (LEVELS - 1))
            ],
            pltpu.SemaphoreType.DMA((12 + 2 * (LEVELS - 1),)),
            pltpu.SemaphoreType.DMA((12 + 2 * (LEVELS - 1),)),
            pltpu.SemaphoreType.DMA((2,)),
        ],
        compiler_params=pltpu.CompilerParams(collective_id=0, has_side_effects=True, vmem_limit_bytes=40 << 20),
    )(x)
    return y.transpose(0, 1, 3, 2, 4).reshape(images, own, cols)


def solution(mesh):
    return jax.shard_map(
        functools.partial(shards, mesh.shape["row"], mesh.shape["col"]),
        mesh=mesh,
        in_specs=(P(None, "row", "col"),),
        out_specs=P(None, "row", "col"),
        check_vma=False,
    )
```

```python
import functools

import jax
import jax.numpy as jnp
from jax import lax
from jax.experimental import pallas as pl
from jax.experimental.pallas import tpu as pltpu
from jax.sharding import PartitionSpec as P

LEVELS = 3
PREDICT_ONE = -1.586134342
UPDATE_ONE = -0.05298011854
PREDICT_TWO = 0.8829110762
UPDATE_TWO = 0.4435068522
SCALE_HIGH = 1.230174105
SCALE_LOW = 1.0 / 1.230174105
STEPS = (PREDICT_ONE, UPDATE_ONE, PREDICT_TWO, UPDATE_TWO)

SUB, LANE = 8, 128
REACH = 4

TRIPS = (16, 16, 8)


def row_level(rows, count, at_top, at_bottom):
    rows = dict(rows)
    for step, factor in enumerate(STEPS):
        for r in range(-REACH + 1 + step, count + REACH - 2 - step, 2):
            before, after = rows[r - 1], rows[r + 1]
            if r == 0:
                before = jnp.where(at_top, after, before)
            if r == count - 1:
                after = jnp.where(at_bottom, before, after)
            rows[r] = rows[r] + factor * (before + after)
    return [rows[r] * (SCALE_HIGH if r % 2 else SCALE_LOW) for r in range(count)]


def lane_levels(group, level, last, masks):
    dist = 1 << level
    lane, at_left, at_right = masks
    first = (lane & dist) == 0
    head, tail = lane < 2 * dist, lane >= LANE - 2 * dist
    mirror_left, mirror_right = at_left & head, at_right & tail
    count = len(group[0])

    def up(t, by):
        return pltpu.roll(t, by, 1)

    def down(t, by):
        return pltpu.roll(t, LANE - by, 1)

    pairs = list(zip(group[::2], group[1::2]))
    even = [[jnp.where(first, x, up(y, dist)) for x, y in zip(*p)] for p in pairs]
    odd = [[jnp.where(first, down(x, dist), y) for x, y in zip(*p)] for p in pairs]
    for step, factor in enumerate(STEPS):
        if step % 2 == 0:
            for s, d in zip(even, odd):
                far = [down(t, 2 * dist) for t in s]
                for q in range(count):
                    after = jnp.where(tail, far[(q + 1) % count], far[q])
                    if q == count - 1:
                        after = jnp.where(mirror_right, s[q], after)
                    d[q] = d[q] + factor * (s[q] + after)
        else:
            for s, d in zip(even, odd):
                far = [up(t, 2 * dist) for t in d]
                for q in range(count):
                    before = jnp.where(head, far[q - 1], far[q])
                    if q == 1:
                        before = jnp.where(mirror_left, d[q], before)
                    s[q] = s[q] + factor * (before + d[q])
    even = [[t * SCALE_LOW for t in s] for s in even]
    result = []
    if level < last:
        for s in lane_levels(even, level + 1, last, masks):
            result += [s, [down(t, dist) for t in s]]
        return result
    for s, d in zip(even, odd):
        d = [t * SCALE_HIGH for t in d]
        result.append([jnp.where(first, x, up(y, dist)) for x, y in zip(s, d)])
        result.append([jnp.where(first, down(x, dist), y) for x, y in zip(s, d)])
    return result


def kernel(nr, nc, x, out, held, done, *rest):
    banks, rest = rest[:LEVELS], rest[LEVELS:]
    edges, (send_sem, recv_sem, out_sem) = rest[:-3], rest[-3:]
    images, bands, tiles = x.shape[0], x.shape[1], x.shape[2]
    half = tiles // 2
    width = half + 2
    own = bands * SUB
    r_at, c_at = lax.axis_index("row"), lax.axis_index("col")

    def inside(dr, dc):
        ok = []
        if dr:
            ok.append(r_at > 0 if dr < 0 else r_at < nr - 1)
        if dc:
            ok.append(c_at > 0 if dc < 0 else c_at < nc - 1)
        return ok[0] if len(ok) == 1 else ok[0] & ok[1]

    around = [(dr, dc) for dr in (-1, 0, 1) for dc in (-1, 0, 1) if dr or dc]
    barrier = pltpu.get_barrier_semaphore()
    total = jnp.int32(0)
    for dr, dc in around:
        ok = inside(dr, dc)
        total = total + ok.astype(jnp.int32)

        @pl.when(ok)
        def _():
            pl.semaphore_signal(
                barrier, inc=1, device_id=(r_at + dr, c_at + dc),
                device_id_type=pl.DeviceIdType.MESH,
            )

    row_part = {
        -1: (pl.ds(bands - 1, 1), pl.ds(0, 1), pl.ds(SUB - REACH, REACH)),
        0: (pl.ds(0, bands), pl.ds(1, bands), pl.ds(0, SUB)),
        1: (pl.ds(0, 1), pl.ds(bands + 1, 1), pl.ds(0, REACH)),
    }
    col_part = (
        (0, 0, pl.ds(0, half + 1), pl.ds(1, half + 1)),
        (0, 1, pl.ds(half - 1, half + 1), pl.ds(0, half + 1)),
        (-1, 0, pl.ds(tiles - 1, 1), pl.ds(0, 1)),
        (1, 1, pl.ds(0, 1), pl.ds(width - 1, 1)),
    )
    parts = [
        (dr, dc, x.at[:, src_r, src_c, subs], held.at[h, :, dst_r, dst_c, subs])
        for dr, (src_r, dst_r, subs) in row_part.items()
        for dc, h, src_c, dst_c in col_part
    ]

    def local(n):
        return pltpu.make_async_copy(parts[n][2], parts[n][3], recv_sem.at[n])

    def remote(n):
        dr, dc, src, dst = parts[n]
        return pltpu.make_async_remote_copy(
            src_ref=src, dst_ref=dst, send_sem=send_sem.at[n], recv_sem=recv_sem.at[n],
            device_id=(r_at - dr, c_at - dc), device_id_type=pl.DeviceIdType.MESH,
        )

    for n, (dr, dc, _, _) in enumerate(parts):
        if not (dr or dc):
            local(n).start()
    pl.semaphore_wait(barrier, total)
    order = sorted(range(len(parts)), key=lambda n: parts[n][1] != 0)
    for n in order:
        dr, dc = parts[n][:2]
        if dr or dc:
            @pl.when(inside(-dr, -dc))
            def _():
                remote(n).start()
    for n, (dr, dc, _, _) in enumerate(parts):
        if dr or dc:
            @pl.when(inside(dr, dc))
            def _():
                remote(n).wait_recv()
        else:
            local(n).wait()

    strands = 2 * images
    pitch = (bands + 2) * width * SUB
    flat = held.reshape(strands * pitch, LANE)
    lane = lax.broadcasted_iota(jnp.int32, (strands, LANE), 1)
    strand = lax.broadcasted_iota(jnp.int32, (strands, LANE), 0)
    at_top = jnp.broadcast_to(r_at == 0, (strands, LANE))
    at_bottom = jnp.broadcast_to(r_at == nr - 1, (strands, LANE))
    at_left = (strand < images) & (c_at == 0)
    at_right = (strand >= images) & (c_at == nc - 1)
    masks = (lane, at_left, at_right)
    stretch = bands * half * SUB
    target = done.reshape(strands * stretch, LANE)

    def fetch(r, t):
        at = r + SUB
        start = ((at // SUB) * width + t) * SUB + at % SUB
        return flat[pl.ds(start, strands, stride=pitch), :]

    def keep(level, rows, q):
        count = own >> level
        found = row_level(rows, count, at_top, at_bottom)
        for r, value in enumerate(found):
            banks[level][r, q] = value
        if level < LEVELS - 1:
            lows = found[::2]
            up, down = edges[4 * level], edges[4 * level + 1]
            for r in range(REACH - 1):
                up[r, q] = lows[r]
            for r in range(REACH):
                down[r, q] = lows[len(lows) - REACH + r]

    cut = half // 2 + 1
    pieces = (pl.ds(0, cut), pl.ds(cut, half + 1 - cut))

    def passing(level, n, piece):
        at = 12 + 4 * level + 2 * n + piece
        part = pieces[piece]
        return pltpu.make_async_remote_copy(
            src_ref=edges[4 * level + n].at[:, part], dst_ref=edges[4 * level + 2 + n].at[:, part],
            send_sem=send_sem.at[at], recv_sem=recv_sem.at[at],
            device_id=(r_at - 1 + 2 * n, c_at), device_id_type=pl.DeviceIdType.MESH,
        )

    def send(level, piece):
        for n in range(2):
            @pl.when(inside(2 * n - 1, 0))
            def _():
                passing(level, n, piece).start()

    def receive(level):
        for n in range(2):
            @pl.when(inside(1 - 2 * n, 0))
            def _():
                passing(level, n, 0).wait_recv()
                passing(level, n, 1).wait_recv()

    span = range(-REACH, own + REACH - 1)
    keep(0, {r: jnp.where(lane < LANE // 2, fetch(r, width - 1), fetch(r, 0)) for r in span}, 0)

    def first_rows(q, carry):
        keep(0, {r: fetch(r, q) for r in span}, q)
        return carry

    lax.fori_loop(1, cut, first_rows, 0)
    send(0, 0)
    lax.fori_loop(cut, half + 1, first_rows, 0)
    send(0, 1)

    for level in range(LEVELS):
        dist = 1 << level
        trip = TRIPS[level]

        def lanes(i, carry):
            group = [
                [banks[level][trip * i + k, q] for q in range(half + 1)] for k in range(trip)
            ]
            group = lane_levels(group, 0, level, masks)
            for k in range(trip):
                r = (trip * i + k) * dist
                for q in range(half):
                    start = ((r // SUB) * half + q) * SUB + r % SUB
                    at = pl.ds(start, strands, stride=stretch)
                    new = group[k][q + 1]
                    if level:
                        new = jnp.where(lane % dist == 0, new, target[at, :])
                    target[at, :] = new
            return carry

        lax.fori_loop(0, (own >> level) // trip, lanes, 0)
        if level < LEVELS - 1:
            receive(level)
            count = own >> (level + 1)

            def next_rows(q, carry):
                rows = {r: banks[level][2 * r, q] for r in range(count)}
                for r in range(REACH):
                    rows[r - REACH] = edges[4 * level + 3][r, q]
                for r in range(REACH - 1):
                    rows[count + r] = edges[4 * level + 2][r, q]
                keep(level + 1, rows, q)
                return carry

            lax.fori_loop(0, cut, next_rows, 0)
            if level + 1 < LEVELS - 1:
                send(level + 1, 0)
            lax.fori_loop(cut, half + 1, next_rows, 0)
            if level + 1 < LEVELS - 1:
                send(level + 1, 1)

    copies = [
        pltpu.make_async_copy(done.at[h], out.at[:, :, pl.ds(h * half, half)], out_sem.at[h])
        for h in range(2)
    ]
    for copy in copies:
        copy.start()
    for n, (dr, dc, _, _) in enumerate(parts):
        if dr or dc:
            @pl.when(inside(-dr, -dc))
            def _():
                remote(n).wait_send()
    for level in range(LEVELS - 1):
        for n in range(2):
            @pl.when(inside(2 * n - 1, 0))
            def _():
                passing(level, n, 0).wait_send()
                passing(level, n, 1).wait_send()
    for copy in copies:
        copy.wait()


def shards(nr, nc, block):
    images, own, cols = block.shape
    bands, tiles = own // SUB, cols // LANE
    half = tiles // 2
    x = block.reshape(images, bands, SUB, tiles, LANE).transpose(0, 1, 3, 2, 4)
    y = pl.pallas_call(
        functools.partial(kernel, nr, nc),
        out_shape=jax.ShapeDtypeStruct(x.shape, x.dtype),
        in_specs=[pl.BlockSpec(memory_space=pltpu.HBM)],
        out_specs=pl.BlockSpec(memory_space=pl.ANY),
        scratch_shapes=[
            pltpu.VMEM((2, images, bands + 2, half + 2, SUB, LANE), jnp.float32),
            pltpu.VMEM((2, images, bands, half, SUB, LANE), jnp.float32),
            *[pltpu.VMEM((own >> n, half + 1, 2 * images, LANE), jnp.float32) for n in range(LEVELS)],
            *[
                pltpu.VMEM((n, half + 1, 2 * images, LANE), jnp.float32)
                for n in (REACH - 1, REACH) * (2 * (LEVELS - 1))
            ],
            pltpu.SemaphoreType.DMA((12 + 4 * (LEVELS - 1),)),
            pltpu.SemaphoreType.DMA((12 + 4 * (LEVELS - 1),)),
            pltpu.SemaphoreType.DMA((2,)),
        ],
        compiler_params=pltpu.CompilerParams(collective_id=0, has_side_effects=True, vmem_limit_bytes=40 << 20),
    )(x)
    return y.transpose(0, 1, 3, 2, 4).reshape(images, own, cols)


def solution(mesh):
    return jax.shard_map(
        functools.partial(shards, mesh.shape["row"], mesh.shape["col"]),
        mesh=mesh,
        in_specs=(P(None, "row", "col"),),
        out_specs=P(None, "row", "col"),
        check_vma=False,
    )
```
